512 devices in a mesh: row: 64 (over x, z, core), col: 8 (over y).
Axes of the slice: x: 4, y: 8, z: 8, core: 2. Of those that a mesh axis runs over, the one named last changes fastest.
Arguments:
- trailing: float32 [32768, 8192], P('row', 'col'), may hold values from -6 to 6
- reflectors: float32 [32768, 256], P('row', 'col'), may hold values from -0.25 to 0.25
- leaf_factor: float32 [16384, 256], P('row', 'col'), may hold values from -0.5 to 0.5
- node_reflect: float32 [6, 16384, 256], P(None, 'row', 'col'), may hold values from -0.375 to 0.375
- node_factor: float32 [6, 16384, 256], P(None, 'row', 'col'), may hold values from -0.5 to 0.5
Outputs:
- updated: float32 [32768, 8192], P('row', 'col')
The draws below stay inside these ranges and needn't reach their ends.
All inputs are finite; a program needn't handle non-finite values.
Results may differ from the reference program's by a relative error of at most 0.00014.
Values sent between devices are 32-bit elements; how exact they have to be, the bound alone decides.
A program may use at most 64 MiB of HBM per device.

```python
import jax
import jax.numpy as jnp
from jax import lax

B = 256
ROWS_DEV = 512
ROWS = 32768
COLS = 8192
SECTIONS = 6
N_ROW = 64


def block_levels(key, shape, pieces, low, largest):
    def one(axis_at, shards_of):
        draws = jax.random.uniform(jax.random.fold_in(jax.random.fold_in(key, 6), axis_at), (shards_of,), jnp.float32, low / len(pieces), largest / len(pieces))
        return jnp.repeat(jnp.exp(draws), shape[axis_at] // shards_of).reshape((-1,) + (1,) * (len(shape) - axis_at - 1))

    level = one(*pieces[0])
    for cut in pieces[1:]:
        level = level * one(*cut)
    return level


def bell_draw(own_key, extent, scale, most, pieces=(), held_as=jnp.bfloat16):
    gain = block_levels(own_key, extent, pieces, -0.22, 0.18) if pieces else 1.0
    values = jax.random.normal(own_key, extent, jnp.float32) * scale * gain
    return jnp.minimum(jnp.maximum(values, -most), most).astype(held_as)


def setup_inputs(seed: int = 0) -> dict:
    splits = jax.random.split(jax.random.key(seed), 6)
    trailing = bell_draw(splits[0], (ROWS, COLS), 1.0, 6.0, ((0, 64), (1, 8)), jnp.float32)
    reflectors = bell_draw(splits[1], (ROWS, B), ROWS_DEV ** -0.5, 0.25, ((0, 64), (1, 8)), jnp.float32)
    leaf_factor = bell_draw(splits[2], (N_ROW * B, B), (0.5 / B ** 0.5), 0.5, ((0, 64), (1, 8)), jnp.float32)
    node_reflect = bell_draw(splits[3], (SECTIONS, N_ROW * B, B), B ** -0.5, 0.375, ((1, 64), (2, 8)), jnp.float32)
    node_factor = bell_draw(splits[4], (SECTIONS, N_ROW * B, B), (0.5 / B ** 0.5), 0.5, ((1, 64), (2, 8)), jnp.float32)
    return {"trailing": trailing, "reflectors": reflectors, "leaf_factor": leaf_factor, "node_reflect": node_reflect, "node_factor": node_factor}


highest = lax.Precision.HIGHEST


def triangle(factor):
    return jnp.triu(factor) + 0.5 * jnp.eye(factor.shape[-1], dtype=factor.dtype)


def reference(trailing, reflectors, leaf_factor, node_reflect, node_factor):
    width = trailing.shape[1]
    matrix = trailing.reshape(N_ROW, ROWS_DEV, width)
    vectors = reflectors.reshape(N_ROW, ROWS_DEV, B)
    leaf_tri = triangle(leaf_factor.reshape(N_ROW, B, B))
    inner = jnp.einsum("nrb,nrc->nbc", vectors, matrix, precision=highest)
    scaled = jnp.einsum("nkb,nkc->nbc", leaf_tri, inner, precision=highest)
    matrix = matrix - jnp.einsum("nrb,nbc->nrc", vectors, scaled, precision=highest)
    uppers = matrix[:, :B]
    remainder = matrix[:, B:]
    for section in range(SECTIONS):
        offset = 2 ** section
        groups = N_ROW // (2 * offset)
        node_y = node_reflect[section].reshape(groups, 2, offset, B, B)[:, 1]
        node_tri = triangle(node_factor[section].reshape(groups, 2, offset, B, B)[:, 0])
        grouped = uppers.reshape(groups, 2, offset, B, width)
        leaders = grouped[:, 0]
        partners = grouped[:, 1]
        summed = leaders + jnp.einsum("gokb,gokc->gobc", node_y, partners, precision=highest)
        coupling = jnp.einsum("gokb,gokc->gobc", node_tri, summed, precision=highest)
        leaders = leaders - coupling
        partners = partners - jnp.einsum("gobk,gokc->gobc", node_y, coupling, precision=highest)
        uppers = jnp.stack([leaders, partners], axis=1).reshape(N_ROW, B, width)
    result = jnp.concatenate([uppers, remainder], axis=1)
    return result.reshape(N_ROW * ROWS_DEV, width)
```

```python
import jax
import jax.numpy as jnp
from jax import lax
from jax.experimental import pallas as pl
from jax.experimental.pallas import tpu as pltpu
from jax.sharding import PartitionSpec as P

B = 256
S = 32
W = 128
MESH = pl.DeviceIdType.MESH
F32 = jnp.float32
BF16 = jnp.bfloat16


def rem(a, b):
    return lax.rem(a, jnp.int32(b))


def div(a, b):
    return lax.div(a, jnp.int32(b))


def swap(v):
    return rem(v, 2) * 2 + div(v, 2)


def split(x):
    hi = x.astype(BF16)
    lo = (x - hi.astype(F32)).astype(BF16)
    return hi, lo


def dot(a, b):
    return jnp.dot(a, b, preferred_element_type=F32)


def mul(stacked, x):
    hi, lo = split(x)
    both = dot(stacked[...], hi)
    return both[:B] + (both[B:] + dot(stacked[:B], lo))


def put(stacked, x):
    hi, lo = split(x)
    stacked[:B] = hi
    stacked[B:] = lo


def triangle(turned):
    row = lax.broadcasted_iota(jnp.int32, (B, B), 0)
    col = lax.broadcasted_iota(jnp.int32, (B, B), 1)
    kept = jnp.where(col <= row, turned, 0.0)
    return kept + jnp.where(col == row, 0.5, 0.0).astype(F32)


def kernel(
    tr, vh, th, nr, nf, out,
    VL, TL, PL, WS, LB, PB, A8, SND, SC, OB, X0, X1, X2, FIN,
    VT, VN, TT, FT, YT, YN,
    ld, lda, ring_s, ring_r, pg_s, pg_r, sib_s, sib_r, late_s, late_r, a_s, a_r, b_s, b_r, c_s, c_r, f_s, f_r, st,
):
    r = lax.axis_index("row")
    y = lax.axis_index("col")
    d0 = rem(r, 4)
    d1 = rem(div(r, 4), 4)
    d2 = div(r, 16)
    core = rem(d0, 2)
    z0 = div(d0, 2)

    def row(a, b, c):
        return a + 4 * b + 16 * c

    right = rem(y + 1, 8)
    left = rem(y + 7, 8)
    sibling = row(d0 + 1 - 2 * core, d1, d2)

    load_v = pltpu.make_async_copy(vh, VL, ld.at[0])
    load_t = pltpu.make_async_copy(th, TL, ld.at[1])
    load_v.start()
    load_t.start()
    bits = [rem(div(r, 1 << s), 2) for s in range(6)]
    for s in range(6):

        @pl.when(bits[s] == 0)
        def _():
            pltpu.make_async_copy(nf.at[s], PL.at[s], ld.at[2 + s]).start()

        @pl.when(bits[s] == 1)
        def _():
            pltpu.make_async_copy(nr.at[s], PL.at[s], ld.at[2 + s]).start()

    for c in range(8):
        pltpu.make_async_copy(tr.at[:, c * W : (c + 1) * W], A8.at[c], lda.at[c]).start()

    barrier = pltpu.get_barrier_semaphore()

    def greet(a, b):
        pl.semaphore_signal(barrier, inc=1, device_id=(a, b), device_id_type=MESH)

    greet(r, right)
    greet(r, left)
    for t in range(1, 4):
        greet(row(rem(d0 + t, 4), d1, d2), y)
        greet(row(d0, rem(d1 + t, 4), d2), y)
        greet(row(d0, d1, rem(d2 + t, 4)), y)
    self_b = d1 == swap(d0)
    back = rem(d2 - d1 + 4, 4)
    self_c = back == d1
    for t in range(4):
        if t:
            greet(row(swap(d1), rem(d1 + t, 4), d2), y)
            greet(row(d0, back, rem(d2 + t, 4)), y)
        else:

            @pl.when(jnp.logical_not(self_b))
            def _():
                greet(row(swap(d1), d1, d2), y)

            @pl.when(jnp.logical_not(self_c))
            def _():
                greet(row(d0, back, d2), y)

    mine = pl.ds(pl.multiple_of(y * S, S), S)
    load_v.wait()
    load_t.wait()
    LB[0, mine, :] = jnp.transpose(VL[:B, :])
    LB[1, mine, :] = jnp.transpose(VL[B:, :])
    LB[2, mine, :] = jnp.transpose(TL[...])

    expected = 2 + 9 + 6 + jnp.where(self_b, 0, 1) + jnp.where(self_c, 0, 1)
    pl.semaphore_wait(barrier, expected)

    def block(q, owner, half):
        start = owner * S + (16 if half == 1 else 0)
        rows = pl.ds(pl.multiple_of(start, 16), S if half is None else 16)
        if q == 0:
            return LB.at[:, rows, :]
        if q == 1:
            return PB.at[0, core, :, rows, :]
        if q == 2:
            return PB.at[1, :, :, rows, :]
        return PB.at[2, :, d2, rows, :]

    def ring(q, way, t):
        owner = rem(y + (8 - t if way == 0 else t), 8)
        ref = block(q, owner, way if t == 3 else None)
        return pltpu.make_async_remote_copy(
            ref, ref, ring_s.at[q, way, t], ring_r.at[q, way, t],
            device_id=(r, right if way == 0 else left), device_id_type=MESH,
        )

    def arrival(q, way, t):
        owner = rem(y + (7 - t if way == 0 else t + 1), 8)
        ref = block(q, owner, way if t == 3 else None)
        return ref, pltpu.make_async_remote_copy(
            ref, ref, ring_s.at[q, way, t], ring_r.at[q, way, t],
            device_id=(r, right if way == 0 else left), device_id_type=MESH,
        )

    def to_sibling(ref, n):
        return pltpu.make_async_remote_copy(
            ref, ref, sib_s.at[n], sib_r.at[n], device_id=(sibling, y), device_id_type=MESH,
        )

    def ring_begin(q):
        for way in range(2):
            ring(q, way, 0).start()
        if q == 1:
            to_sibling(block(1, y, None), 8).start()

    def ring_step(q, t):
        for way in range(2):
            ref, copy = arrival(q, way, t)
            copy.wait_recv()
            if t < 3:
                ring(q, way, t + 1).start()
            if q == 1:
                to_sibling(ref, 2 * t + way).start()

    ring_begin(0)

    for s in range(6):
        pltpu.make_async_copy(nf.at[s], PL.at[s], ld.at[2 + s]).wait()
        WS[s] = jnp.transpose(PL[s])

    def pre0(level, side):
        to = level + 2 * side
        return pltpu.make_async_remote_copy(
            WS.at[level], PB.at[0, level, d0, mine, :], pg_s.at[2 * level + side], pg_r.at[d0],
            device_id=(row(jnp.int32(to), d1, d2), y), device_id_type=MESH,
        )

    def pre0_own(level):
        return pltpu.make_async_copy(WS.at[level], PB.at[0, level, d0, mine, :], pg_r.at[d0])

    for level in range(2):
        for side in range(2):

            @pl.when(d0 != level + 2 * side)
            def _():
                pre0(level, side).start()

            @pl.when(d0 == level + 2 * side)
            def _():
                pre0_own(level).start()

    def pre1(t):
        return pltpu.make_async_remote_copy(
            WS.at[2:4], PB.at[1, :, d1, mine, :], pg_s.at[4 + t], pg_r.at[4 + d1],
            device_id=(row(d0, rem(d1 + t, 4), d2), y), device_id_type=MESH,
        )

    for t in (2, 1, 3):
        pre1(t).start()
    own1 = pltpu.make_async_copy(WS.at[2:4], PB.at[1, :, d1, mine, :], pg_r.at[4 + d1])
    own1.start()
    own2 = pltpu.make_async_copy(WS.at[4:6], PB.at[2, :, d2, mine, :], pg_r.at[8])
    own2.start()

    def pre0_wait():
        for j in range(4):
            pltpu.make_async_copy(WS.at[0], PB.at[0, core, j, mine, :], pg_r.at[j]).wait()

    def pre1_wait():
        for j in range(4):
            pltpu.make_async_copy(WS.at[2:4], PB.at[1, :, j, mine, :], pg_r.at[4 + j]).wait()

    ring_step(0, 0)
    ring_step(0, 1)
    pre0_wait()
    ring_begin(1)
    ring_step(0, 2)
    ring_step(0, 3)

    for n in range(2):
        flat = LB[n]
        put(VT.at[n], flat)
        put(VN.at[n], jnp.transpose(flat))
    put(TT, triangle(LB[2]))
    ring_step(1, 0)

    def spread(k):
        other = 2 - 2 * z0
        return jnp.where(
            k == 0, other + core, jnp.where(k == 1, other + 1 - core, jnp.where(k == 2, 2 * z0 + 1 - core, d0))
        )

    def a_copy(h, k):
        to = spread(k)
        chunk = 2 * to + h
        return pltpu.make_async_remote_copy(
            SND.at[chunk], X0.at[h, d0], a_s.at[h, k], a_r.at[h, d0],
            device_id=(row(to, d1, d2), y), device_id_type=MESH,
        )

    def leaf(h):
        def body(k, _):
            chunk = 2 * spread(k) + h
            pltpu.make_async_copy(tr.at[:, 0:W], A8.at[chunk], lda.at[chunk]).wait()
            upper = A8[chunk, :B, :]
            lower = A8[chunk, B:, :]
            inner = mul(VT.at[0], upper) + mul(VT.at[1], lower)
            scaled = mul(TT, inner)
            SC[chunk] = scaled
            SND[chunk] = upper - mul(VN.at[0], scaled)

            @pl.when(k < 3)
            def _():
                a_copy(h, k).start()

            @pl.when(k == 3)
            def _():
                pltpu.make_async_copy(SND.at[chunk], X0.at[h, d0], a_r.at[h, d0]).start()

            return 0

        lax.fori_loop(0, 4, body, 0)

    leaf(0)
    ring_step(1, 1)
    leaf(1)
    ring_step(1, 2)
    pre1_wait()
    ring_begin(2)

    def remainder(chunk, _):
        OB[chunk] = A8[chunk, B:, :] - mul(VN.at[1], SC[chunk])
        pltpu.make_async_copy(
            OB.at[chunk], out.at[B:, pl.ds(pl.multiple_of(chunk * W, W), W)], st.at[chunk]
        ).start()
        return 0

    lax.fori_loop(0, 8, remainder, 0)
    ring_step(1, 3)
    own2.wait()

    def sibling_wait():
        other = PB.at[0, 1 - core]
        for n in range(8):
            way, t = n % 2, n // 2
            owner = rem(y + (7 - t if way == 0 else t + 1), 8)
            start = owner * S + (16 if t == 3 and way == 1 else 0)
            rows = pl.ds(pl.multiple_of(start, 16), S if t < 3 else 16)
            ref = other.at[:, rows, :]
            to_sibling(ref, n).wait_recv()
        to_sibling(other.at[:, mine, :], 8).wait_recv()

    def prepare(q):
        def body(e, _):
            level, n = div(e, 2), rem(e, 2)
            k = (2 - level) * n
            p = k + 1 + level
            put(FT.at[e], triangle(PB[q, level, k]))
            turned = PB[q, level, p]
            put(YT.at[e], turned)
            put(YN.at[e], jnp.transpose(turned))
            return 0

        lax.fori_loop(0, 4, body, 0)

    def apply(X, h):
        def body(level, _):
            at = [((2 - level) * n, (2 - level) * n + 1 + level) for n in range(2)]
            for n in range(2):
                k, p = at[n]
                e = 2 * level + n
                lead = X[h, k]
                follow = X[h, p]
                summed = lead + mul(YT.at[e], follow)
                coupling = mul(FT.at[e], summed)
                X[h, k] = lead - coupling
                X[h, p] = follow - mul(YN.at[e], coupling)
            return 0

        lax.fori_loop(0, 2, body, 0)

    def tops_wait(X, sem, h):
        for j in range(4):
            pltpu.make_async_copy(X.at[h, j], X.at[h, j], sem.at[h, j]).wait()

    def b_copy(h, t):
        i = rem(d0 + t, 4)
        return pltpu.make_async_remote_copy(
            X0.at[h, i], X1.at[h, d1], b_s.at[h, t], b_r.at[h, d1],
            device_id=(row(i, swap(d0), d2), y), device_id_type=MESH,
        )

    def c_copy(h, t):
        i = rem(d1 + t, 4)
        return pltpu.make_async_remote_copy(
            X1.at[h, i], X2.at[h, d2], c_s.at[h, t], c_r.at[h, d2],
            device_id=(row(d0, i, rem(d1 + i, 4)), y), device_id_type=MESH,
        )

    to_self_c = rem(d1 + d1, 4) == d2

    def f_copy(h, t):
        i = rem(d2 + t, 4)
        return pltpu.make_async_remote_copy(
            X2.at[h, i], FIN.at[h, d2], f_s.at[h, t], f_r.at[h, d2],
            device_id=(row(d0, d1, i), y), device_id_type=MESH,
        )

    def send(copy, h, own, local):
        for t in (2, 1, 3):
            copy(h, t).start()
        if own is None:
            local.start()
        else:

            @pl.when(jnp.logical_not(own))
            def _():
                copy(h, 0).start()

            @pl.when(own)
            def _():
                local.start()

    sibling_wait()
    prepare(0)
    ring_step(2, 0)
    for h in range(2):
        tops_wait(X0, a_r, h)
        apply(X0, h)
        send(b_copy, h, self_b, pltpu.make_async_copy(X0.at[h, d0], X1.at[h, d1], b_r.at[h, d1]))
        if h == 0:
            ring_step(2, 1)
            ring_begin(3)
    ring_step(2, 2)
    ring_step(2, 3)
    prepare(1)
    for t in range(3):
        ring_step(3, t)

    def late(t):
        return pltpu.make_async_remote_copy(
            PB.at[2, :, d2], PB.at[2, :, d2], late_s.at[t], late_r.at[d2],
            device_id=(row(d0, d1, rem(d2 + t, 4)), y), device_id_type=MESH,
        )

    for h in range(2):
        tops_wait(X1, b_r, h)
        apply(X1, h)
        send(c_copy, h, to_self_c, pltpu.make_async_copy(X1.at[h, d1], X2.at[h, d2], c_r.at[h, d2]))
        if h == 0:
            ring_step(3, 3)
            for t in (2, 1, 3):
                late(t).start()

    for t in range(1, 4):
        j = rem(d2 + t, 4)
        pltpu.make_async_copy(PB.at[2, :, j], PB.at[2, :, j], late_r.at[j]).wait()
    prepare(2)

    for h in range(2):
        tops_wait(X2, c_r, h)
        apply(X2, h)
        send(f_copy, h, None, pltpu.make_async_copy(X2.at[h, d2], FIN.at[h, d2], f_r.at[h, d2]))

    def home(h, j):
        quarter = swap(rem(j - d1 + 4, 4))
        cols = pl.ds(pl.multiple_of(quarter * 256 + h * W, W), W)
        return pltpu.make_async_copy(FIN.at[h, j], out.at[:B, cols], st.at[8 + 4 * h + j])

    for h in range(2):
        for j in range(4):
            pltpu.make_async_copy(FIN.at[h, j], FIN.at[h, j], f_r.at[h, j]).wait()
            home(h, j).start()

    for q in range(4):
        for way in range(2):
            for t in range(4):
                ring(q, way, t).wait_send()
    for n in range(8):
        ref, _ = arrival(1, n % 2, n // 2)
        to_sibling(ref, n).wait_send()
    to_sibling(block(1, y, None), 8).wait_send()
    for level in range(2):
        for side in range(2):

            @pl.when(d0 != level + 2 * side)
            def _():
                pre0(level, side).wait_send()

    for t in range(1, 4):
        pre1(t).wait_send()
        late(t).wait_send()
    for h in range(2):
        for k in range(3):
            a_copy(h, k).wait_send()
        for t in range(1, 4):
            b_copy(h, t).wait_send()
            c_copy(h, t).wait_send()
            f_copy(h, t).wait_send()

        @pl.when(jnp.logical_not(self_b))
        def _():
            b_copy(h, 0).wait_send()

        @pl.when(jnp.logical_not(to_self_c))
        def _():
            c_copy(h, 0).wait_send()

    for chunk in range(8):
        pltpu.make_async_copy(OB.at[chunk], out.at[B:, chunk * W : (chunk + 1) * W], st.at[chunk]).wait()
    for h in range(2):
        for j in range(4):
            home(h, j).wait()


def per_device(trailing, reflectors, leaf_factor, node_reflect, node_factor):
    anywhere = pl.BlockSpec(memory_space=pl.ANY)
    dma = pltpu.SemaphoreType.DMA
    tops = pltpu.VMEM((2, 4, B, W), F32)
    nodes = pltpu.VMEM((4, 2 * B, B), BF16)
    return pl.pallas_call(
        kernel,
        out_shape=jax.ShapeDtypeStruct(trailing.shape, F32),
        in_specs=[anywhere] * 5,
        out_specs=anywhere,
        scratch_shapes=[
            pltpu.VMEM((2 * B, S), F32),
            pltpu.VMEM((B, S), F32),
            pltpu.VMEM((6, B, S), F32),
            pltpu.VMEM((6, S, B), F32),
            pltpu.VMEM((3, B, B), F32),
            pltpu.VMEM((3, 2, 4, B, B), F32),
            pltpu.VMEM((8, 2 * B, W), F32),
            pltpu.VMEM((8, B, W), F32),
            pltpu.VMEM((8, B, W), F32),
            pltpu.VMEM((8, B, W), F32),
            tops, tops, tops, tops,
            pltpu.VMEM((2, 2 * B, B), BF16),
            pltpu.VMEM((2, 2 * B, B), BF16),
            pltpu.VMEM((2 * B, B), BF16),
            nodes, nodes, nodes,
            dma((8,)), dma((8,)),
            dma((4, 2, 4)), dma((4, 2, 4)),
            dma((8,)), dma((9,)),
            dma((9,)), dma((9,)),
            dma((4,)), dma((4,)),
            dma((2, 4)), dma((2, 4)),
            dma((2, 4)), dma((2, 4)),
            dma((2, 4)), dma((2, 4)),
            dma((2, 4)), dma((2, 4)),
            dma((16,)),
        ],
        compiler_params=pltpu.CompilerParams(
            collective_id=0, has_side_effects=True, vmem_limit_bytes=56 * 1024 * 1024
        ),
        name="update",
    )(trailing, reflectors, leaf_factor, node_reflect, node_factor)


def solution(mesh):
    in_specs = (
        P("row", "col"),
        P("row", "col"),
        P("row", "col"),
        P(None, "row", "col"),
        P(None, "row", "col"),
    )
    return jax.shard_map(
        per_device, mesh=mesh, in_specs=in_specs, out_specs=P("row", "col"), check_vma=False
    )
```

```python
import jax
import jax.numpy as jnp
from jax import lax
from jax.experimental import pallas as pl
from jax.experimental.pallas import tpu as pltpu
from jax.sharding import PartitionSpec as P

B = 256
S = 32
W = 128
SHARED = (3, 4, 6, 7)
MESH = pl.DeviceIdType.MESH
F32 = jnp.float32
BF16 = jnp.bfloat16


def rem(a, b):
    return lax.rem(a, jnp.int32(b))


def div(a, b):
    return lax.div(a, jnp.int32(b))


def split(x):
    hi = x.astype(BF16)
    lo = (x - hi.astype(F32)).astype(BF16)
    return hi, lo


def dot(a, b):
    return jnp.dot(a, b, preferred_element_type=F32)


def mul(stacked, x):
    hi, lo = split(x)
    both = dot(stacked[...], hi)
    return both[:B] + (both[B:] + dot(stacked[:B], lo))


def narrow(stacked, x):
    both = dot(stacked[...], jnp.concatenate(split(x), axis=1))
    return both[:B, :W] + (both[:B, W:] + both[B:, :W])


def put(stacked, x):
    hi, lo = split(x)
    stacked[:B] = hi
    stacked[B:] = lo


def triangle(turned):
    row = lax.broadcasted_iota(jnp.int32, (B, B), 0)
    col = lax.broadcasted_iota(jnp.int32, (B, B), 1)
    kept = jnp.where(col <= row, turned, 0.0)
    return kept + jnp.where(col == row, 0.5, 0.0).astype(F32)


def kernel(
    tr, vh, th, nr, nf, top_out, low_out,
    WS, LB, PB, A4, SND, SC, OB, X0, X1, X2,
    VT, VN, TT, FT, YT, YN,
    ld, lda, ring_s, ring_r, pg_s, pg_r, sib_s, sib_r, late_s, late_r, top_s, top_r, st,
):
    r = lax.axis_index("row")
    y = lax.axis_index("col")
    d0 = rem(r, 4)
    d1 = rem(div(r, 4), 4)
    d2 = div(r, 16)
    core = rem(d0, 2)
    z0 = div(d0, 2)
    z1 = rem(d1, 2)
    z2 = div(d1, 2)

    def row(a, b, c):
        return a + 4 * b + 16 * c

    right = rem(y + 1, 8)
    left = rem(y + 7, 8)
    sibling = row(d0 + 1 - 2 * core, d1, d2)

    mine = pl.ds(pl.multiple_of(y * S, S), S)

    pltpu.make_async_copy(vh.at[:, :B], LB.at[0, mine, :], ld.at[0]).start()
    pltpu.make_async_copy(vh.at[:, B:], LB.at[1, mine, :], ld.at[0]).start()
    pltpu.make_async_copy(th, LB.at[2, mine, :], ld.at[0]).start()
    bits = [rem(div(r, 1 << s), 2) for s in range(6)]
    for s in range(6):

        @pl.when(bits[s] == 0)
        def _():
            pltpu.make_async_copy(nf.at[s], WS.at[s], ld.at[1]).start()

        @pl.when(bits[s] == 1)
        def _():
            pltpu.make_async_copy(nr.at[s], WS.at[s], ld.at[1]).start()

    for c in range(4):
        pltpu.make_async_copy(tr.at[:, c * B : (c + 1) * B], A4.at[c], lda.at[c]).start()

    barrier = pltpu.get_barrier_semaphore()

    def greet(a, b):
        pl.semaphore_signal(barrier, inc=1, device_id=(a, b), device_id_type=MESH)

    greet(r, right)
    greet(r, left)
    for t in range(1, 4):
        greet(row(rem(d0 + t, 4), d1, d2), y)
        greet(row(d0, d1, rem(d2 + t, 4)), y)
    held = rem(d2 - d1 + 4, 4)
    self_a = z2 == core
    self_b = z1 == z0
    self_c = jnp.logical_and(self_a, held == core + 2 * z1)
    for t in range(4):
        sources = (
            (self_a, row(z2 + 2 * z0, rem(d1 + t, 4), d2)),
            (self_b, row(core + 2 * z1, rem(d1 + t, 4), d2)),
            (self_c, row(rem(held, 2) + 2 * z0, div(held, 2) + 2 * core, rem(d2 + t, 4))),
        )
        for own, source in sources:
            if t:
                greet(source, y)
            else:

                @pl.when(jnp.logical_not(own))
                def _():
                    greet(source, y)

    def arrived(ref, sem):
        pltpu.make_async_copy(ref, ref, sem).wait()

    arrived(LB.at[:, mine, :], ld.at[0])
    expected = 8 + 9
    for own in (self_a, self_b, self_c):
        expected = expected + jnp.where(own, 0, 1)
    pl.semaphore_wait(barrier, expected)

    def block(q, owner, half):
        start = owner * S + (16 if half == 1 else 0)
        rows = pl.ds(pl.multiple_of(start, 16), S if half is None else 16)
        if q < 3:
            return LB.at[q, rows, :]
        if q < 5:
            return PB.at[0, core, 2 * (q - 3) : 2 * (q - 2), rows, :]
        if q == 5:
            return PB.at[2, :, d2, rows, :]
        return PB.at[1, core, 2 * (q - 6) : 2 * (q - 5), rows, :]

    def ring(q, way, t):
        owner = rem(y + (8 - t if way == 0 else t), 8)
        ref = block(q, owner, way if t == 3 else None)
        return pltpu.make_async_remote_copy(
            ref, ref, ring_s.at[q], ring_r.at[q, way, t],
            device_id=(r, right if way == 0 else left), device_id_type=MESH,
        )

    def arrival(q, way, t):
        owner = rem(y + (7 - t if way == 0 else t + 1), 8)
        ref = block(q, owner, way if t == 3 else None)
        return ref

    def to_sibling(ref, q):
        return pltpu.make_async_remote_copy(
            ref, ref, sib_s.at[q], sib_r.at[q], device_id=(sibling, y), device_id_type=MESH,
        )

    def ring_begin(q):
        for way in range(2):
            ring(q, way, 0).start()
        if q in SHARED:
            to_sibling(block(q, y, None), q).start()

    def ring_step(q, t):
        for way in range(2):
            ref = arrival(q, way, t)
            arrived(ref, ring_r.at[q, way, t])
            if t < 3:
                ring(q, way, t + 1).start()
            if q in SHARED:
                to_sibling(ref, q).start()

    for q in range(3):
        ring_begin(q)
    arrived(WS, ld.at[1])

    def pre0(level, side):
        to = level + 2 * side
        return pltpu.make_async_remote_copy(
            WS.at[level], PB.at[0, level, d0, mine, :], pg_s.at[0], pg_r.at[0],
            device_id=(row(jnp.int32(to), d1, d2), y), device_id_type=MESH,
        )

    def pre0_own(level):
        return pltpu.make_async_copy(WS.at[level], PB.at[0, level, d0, mine, :], pg_r.at[0])

    for level in range(2):
        for side in range(2):

            @pl.when(d0 != level + 2 * side)
            def _():
                pre0(level, side).start()

            @pl.when(d0 == level + 2 * side)
            def _():
                pre0_own(level).start()

    def pre1(level, side):
        return pltpu.make_async_remote_copy(
            WS.at[2 + level], PB.at[1, level, d1, mine, :], pg_s.at[1], pg_r.at[1],
            device_id=(row(level + 2 * z0, side + 2 * core, d2), y), device_id_type=MESH,
        )

    def pre1_own(level, side):
        return jnp.logical_and(self_a, jnp.logical_and(core == level, z1 == side))

    for level in range(2):
        for side in range(2):

            @pl.when(jnp.logical_not(pre1_own(level, side)))
            def _():
                pre1(level, side).start()

            @pl.when(pre1_own(level, side))
            def _():
                pltpu.make_async_copy(WS.at[2 + level], PB.at[1, level, d1, mine, :], pg_r.at[1]).start()

    own2 = pltpu.make_async_copy(WS.at[4:6], PB.at[2, :, d2, mine, :], pg_r.at[2])
    own2.start()

    for t in range(2):
        for q in range(3):
            ring_step(q, t)
    arrived(PB.at[0, core, :, mine, :], pg_r.at[0])
    for q in range(3):
        ring_step(q, 2)
    ring_begin(3)
    ring_begin(4)
    own2.wait()
    ring_begin(5)
    for n in range(2):
        ring_step(n, 3)
        flat = LB[n]
        put(VT.at[n], flat)
        put(VN.at[n], jnp.transpose(flat))
    ring_step(2, 3)
    put(TT, triangle(LB[2]))

    def spread(k):
        other = 2 - 2 * z0
        return jnp.where(
            k == 0, other + core, jnp.where(k == 1, other + 1 - core, jnp.where(k == 2, 2 * z0 + 1 - core, d0))
        )

    def a_copy(h, k):
        to = spread(k)
        return pltpu.make_async_remote_copy(
            SND.at[to, h], X0.at[h, d0], top_s.at[0], top_r.at[0, h],
            device_id=(row(to, d1, d2), y), device_id_type=MESH,
        )

    def leaf(pair, _):
        quarters = [spread(2 * pair), spread(2 * pair + 1)]
        for quarter in quarters:
            pltpu.make_async_copy(tr.at[:, 0:B], A4.at[quarter], lda.at[quarter]).wait()
        scaled = []
        for quarter in quarters:
            inner = mul(VT.at[0], A4[quarter, :B, :]) + mul(VT.at[1], A4[quarter, B:, :])
            scaled.append(mul(TT, inner))
        for quarter, value in zip(quarters, scaled):
            SC[quarter] = value
            leafed = A4[quarter, :B, :] - mul(VN.at[0], value)
            SND[quarter, 0] = leafed[:, :W]
            SND[quarter, 1] = leafed[:, W:]
        for h in range(2):
            a_copy(h, 2 * pair).start()

            @pl.when(pair == 0)
            def _():
                a_copy(h, 2 * pair + 1).start()

            @pl.when(pair == 1)
            def _():
                pltpu.make_async_copy(SND.at[d0, h], X0.at[h, d0], top_r.at[0, h]).start()

        return 0

    def remainder(quarter, _):
        OB[quarter] = A4[quarter, B:, :] - mul(VN.at[1], SC[quarter])
        pltpu.make_async_copy(
            OB.at[quarter], low_out.at[:, pl.ds(pl.multiple_of(quarter * B, B), B)], st
        ).start()
        return 0

    lax.fori_loop(0, 1, leaf, 0)
    ring_step(3, 0)
    ring_step(4, 0)
    lax.fori_loop(1, 2, leaf, 0)
    ring_step(3, 1)
    ring_step(4, 1)
    ring_step(5, 0)
    lax.fori_loop(0, 1, remainder, 0)
    ring_step(3, 2)
    ring_step(4, 2)
    ring_step(5, 1)
    arrived(PB.at[1, core, :, mine, :], pg_r.at[1])
    ring_begin(6)
    ring_step(3, 3)
    ring_step(4, 3)
    ring_step(5, 2)
    ring_begin(7)

    def sibling_wait(phase):
        for part in range(2):
            arrived(PB.at[phase, 1 - core, 2 * part : 2 * part + 2], sib_r.at[SHARED[2 * phase + part]])

    def prepare(q):
        def body(e, _):
            level, n = div(e, 2), rem(e, 2)
            k = (2 - level) * n
            p = k + 1 + level
            put(FT.at[e], triangle(PB[q, level, k]))
            turned = PB[q, level, p]
            put(YT.at[e], turned)
            put(YN.at[e], jnp.transpose(turned))
            return 0

        lax.fori_loop(0, 4, body, 0)

    def apply(X, h):
        def body(level, _):
            at = [((2 - level) * n, (2 - level) * n + 1 + level) for n in range(2)]
            for n in range(2):
                k, p = at[n]
                e = 2 * level + n
                lead = X[h, k]
                follow = X[h, p]
                summed = lead + narrow(YT.at[e], follow)
                coupling = narrow(FT.at[e], summed)
                X[h, k] = lead - coupling
                X[h, p] = follow - narrow(YN.at[e], coupling)
            return 0

        lax.fori_loop(0, 2, body, 0)

    kept_b = z2 + 2 * z0

    def b_copy(h, t):
        i = rem(kept_b + t, 4)
        return pltpu.make_async_remote_copy(
            X0.at[h, i], X1.at[h, d1], top_s.at[1], top_r.at[1, h],
            device_id=(row(core + 2 * div(i, 2), z0 + 2 * rem(i, 2), d2), y), device_id_type=MESH,
        )

    def c_copy(h, t):
        i = rem(d1 + t, 4)
        return pltpu.make_async_remote_copy(
            X1.at[h, i], X2.at[h, d2], top_s.at[2], top_r.at[2, h],
            device_id=(row(z2 + 2 * z0, i, rem(core + 2 * z1 + i, 4)), y), device_id_type=MESH,
        )

    def home(h):
        quarter = rem(d2 - d1 + 4, 4)
        return top_out.at[:, pl.ds(pl.multiple_of(quarter * B + h * W, W), W)]

    def f_copy(h, t):
        i = rem(d2 + t, 4)
        return pltpu.make_async_remote_copy(
            X2.at[h, i], home(h), top_s.at[3], top_r.at[3, h],
            device_id=(row(d0, d1, i), y), device_id_type=MESH,
        )

    def send(copy, h, own, local):
        for t in (2, 1, 3):
            copy(h, t).start()
        if own is None:
            local().start()
        else:

            @pl.when(jnp.logical_not(own))
            def _():
                copy(h, 0).start()

            @pl.when(own)
            def _():
                local().start()

    def late(t):
        return pltpu.make_async_remote_copy(
            PB.at[2, :, d2], PB.at[2, :, d2], late_s, late_r,
            device_id=(row(d0, d1, rem(d2 + t, 4)), y), device_id_type=MESH,
        )

    sibling_wait(0)
    prepare(0)
    for h in range(2):
        arrived(X0.at[h], top_r.at[0, h])
        apply(X0, h)
        send(b_copy, h, self_b, lambda: pltpu.make_async_copy(X0.at[h, kept_b], X1.at[h, d1], top_r.at[1, h]))
        if h == 0:
            ring_step(5, 3)
            for t in (2, 1, 3):
                late(t).start()
            ring_step(6, 0)
            ring_step(7, 0)
    ring_step(6, 1)
    ring_step(7, 1)
    lax.fori_loop(1, 4, remainder, 0)
    ring_step(6, 2)
    ring_step(7, 2)
    ring_step(6, 3)
    ring_step(7, 3)
    sibling_wait(1)
    prepare(1)


    for h in range(2):
        arrived(X1.at[h], top_r.at[1, h])
        apply(X1, h)
        send(c_copy, h, self_c, lambda: pltpu.make_async_copy(X1.at[h, d1], X2.at[h, d2], top_r.at[2, h]))

    arrived(PB.at[2, :, 0:3], late_r)
    prepare(2)

    for h in range(2):
        arrived(X2.at[h], top_r.at[2, h])
        apply(X2, h)
        send(f_copy, h, None, lambda: pltpu.make_async_copy(X2.at[h, d2], home(h), top_r.at[3, h]))

    for h in range(2):
        arrived(top_out.at[:, 0 : 4 * W], top_r.at[3, h])

    for q in range(8):
        rows = pl.ds(0, 7 * S)
        arrived(LB.at[q, rows] if q < 3 else PB.at[0, 0, 0:2, rows], ring_s.at[q])
    for q in SHARED:
        arrived(PB.at[0, 0, 0:2], sib_s.at[q])
    arrived(WS.at[0:3], pg_s.at[0])
    arrived(PB.at[2, :, 0:3], late_s)
    arrived(X0.at[:, 0:3], top_s.at[0])
    arrived(X0.at[:, 0:3], top_s.at[3])
    for own, sem, few, all_ in (
        (self_a, pg_s.at[1], WS.at[0:3], WS.at[0:4]),
        (self_b, top_s.at[1], X0.at[:, 0:3], X0),
        (self_c, top_s.at[2], X1.at[:, 0:3], X1),
    ):

        @pl.when(own)
        def _():
            arrived(few, sem)

        @pl.when(jnp.logical_not(own))
        def _():
            arrived(all_, sem)

    arrived(OB, st)


def per_device(trailing, reflectors, leaf_factor, node_reflect, node_factor):
    anywhere = pl.BlockSpec(memory_space=pl.ANY)
    dma = pltpu.SemaphoreType.DMA
    tops = pltpu.VMEM((2, 4, B, W), F32)
    nodes = pltpu.VMEM((4, 2 * B, B), BF16)
    half = jax.ShapeDtypeStruct((B, trailing.shape[1]), F32)
    top, low = pl.pallas_call(
        kernel,
        out_shape=(half, half),
        in_specs=[anywhere] * 5,
        out_specs=(anywhere, anywhere),
        scratch_shapes=[
            pltpu.VMEM((6, S, B), F32),
            pltpu.VMEM((3, B, B), F32),
            pltpu.VMEM((3, 2, 4, B, B), F32),
            pltpu.VMEM((4, 2 * B, B), F32),
            pltpu.VMEM((4, 2, B, W), F32),
            pltpu.VMEM((4, B, B), F32),
            pltpu.VMEM((4, B, B), F32),
            tops, tops, tops,
            pltpu.VMEM((2, 2 * B, B), BF16),
            pltpu.VMEM((2, 2 * B, B), BF16),
            pltpu.VMEM((2 * B, B), BF16),
            nodes, nodes, nodes,
            dma((2,)), dma((4,)),
            dma((8,)), dma((8, 2, 4)),
            dma((2,)), dma((3,)),
            dma((8,)), dma((8,)),
            dma, dma,
            dma((4,)), dma((4, 2)),
            dma,
        ],
        compiler_params=pltpu.CompilerParams(
            collective_id=0, has_side_effects=True, vmem_limit_bytes=56 * 1024 * 1024
        ),
        name="update",
    )(
        trailing,
        reflectors.T,
        leaf_factor.T,
        jnp.swapaxes(node_reflect, 1, 2),
        jnp.swapaxes(node_factor, 1, 2),
    )
    return jnp.concatenate([top, low], axis=0)


def solution(mesh):
    in_specs = (
        P("row", "col"),
        P("row", "col"),
        P("row", "col"),
        P(None, "row", "col"),
        P(None, "row", "col"),
    )
    return jax.shard_map(
        per_device, mesh=mesh, in_specs=in_specs, out_specs=P("row", "col"), check_vma=False
    )
```

```python
import jax
import jax.numpy as jnp
from jax import lax
from jax.experimental import pallas as pl
from jax.experimental.pallas import tpu as pltpu
from jax.sharding import PartitionSpec as P

B = 256
S = 32
W = 128
SHARED = (3, 4, 6, 7)
MESH = pl.DeviceIdType.MESH
F32 = jnp.float32
BF16 = jnp.bfloat16


def rem(a, b):
    return lax.rem(a, jnp.int32(b))


def div(a, b):
    return lax.div(a, jnp.int32(b))


def split(x):
    hi = x.astype(BF16)
    lo = (x - hi.astype(F32)).astype(BF16)
    return hi, lo


def dot(a, b):
    return jnp.dot(a, b, preferred_element_type=F32)


def mul(stacked, x):
    both = dot(stacked[...], jnp.concatenate(split(x), axis=1))
    return both[:B, :W] + (both[:B, W:] + both[B:, :W])


def put(stacked, x):
    hi, lo = split(x)
    stacked[:B] = hi
    stacked[B:] = lo


def triangle(turned):
    row = lax.broadcasted_iota(jnp.int32, (B, B), 0)
    col = lax.broadcasted_iota(jnp.int32, (B, B), 1)
    kept = jnp.where(col <= row, turned, 0.0)
    return kept + jnp.where(col == row, 0.5, 0.0).astype(F32)


def kernel(
    tr, vh, th, nr, nf, out,
    WS, LB, PB, A4, SND, SC, X0, X1, X2,
    VT, VN, TT, FT, YT, YN,
    ld, lda, ring_s, ring_r, pg_s, pg_r, sib_s, sib_r, late_s, late_r, top_s, top_r,
):
    r = lax.axis_index("row")
    y = lax.axis_index("col")
    d0 = rem(r, 4)
    d1 = rem(div(r, 4), 4)
    d2 = div(r, 16)
    core = rem(d0, 2)
    z0 = div(d0, 2)
    z1 = rem(d1, 2)
    z2 = div(d1, 2)

    def row(a, b, c):
        return a + 4 * b + 16 * c

    right = rem(y + 1, 8)
    left = rem(y + 7, 8)
    sibling = row(d0 + 1 - 2 * core, d1, d2)

    mine = pl.ds(pl.multiple_of(y * S, S), S)

    pltpu.make_async_copy(vh.at[:, :B], LB.at[0, mine, :], ld.at[0]).start()
    pltpu.make_async_copy(vh.at[:, B:], LB.at[1, mine, :], ld.at[0]).start()
    pltpu.make_async_copy(th, LB.at[2, mine, :], ld.at[0]).start()
    bits = [rem(div(r, 1 << s), 2) for s in range(6)]
    for s in range(6):

        @pl.when(bits[s] == 0)
        def _():
            pltpu.make_async_copy(nf.at[s], WS.at[s], ld.at[1]).start()

        @pl.when(bits[s] == 1)
        def _():
            pltpu.make_async_copy(nr.at[s], WS.at[s], ld.at[1]).start()

    for c in range(4):
        pltpu.make_async_copy(tr.at[:, c * B : (c + 1) * B], A4.at[c], lda).start()

    barrier = pltpu.get_barrier_semaphore()

    def greet(a, b):
        pl.semaphore_signal(barrier, inc=1, device_id=(a, b), device_id_type=MESH)

    greet(r, right)
    greet(r, left)
    for t in range(1, 4):
        greet(row(rem(d0 + t, 4), d1, d2), y)
        greet(row(d0, d1, rem(d2 + t, 4)), y)
    held = rem(d2 - d1 + 4, 4)
    self_a = z2 == core
    self_b = z1 == z0
    self_c = jnp.logical_and(self_a, held == core + 2 * z1)
    for t in range(4):
        sources = (
            (self_a, row(z2 + 2 * z0, rem(d1 + t, 4), d2)),
            (self_b, row(core + 2 * z1, rem(d1 + t, 4), d2)),
            (self_c, row(rem(held, 2) + 2 * z0, div(held, 2) + 2 * core, rem(d2 + t, 4))),
        )
        for own, source in sources:
            if t:
                greet(source, y)
            else:

                @pl.when(jnp.logical_not(own))
                def _():
                    greet(source, y)

    def arrived(ref, sem):
        pltpu.make_async_copy(ref, ref, sem).wait()

    arrived(LB.at[:, mine, :], ld.at[0])
    expected = 8 + 9
    for own in (self_a, self_b, self_c):
        expected = expected + jnp.where(own, 0, 1)
    pl.semaphore_wait(barrier, expected)

    def block(q, owner, half):
        start = owner * S + (16 if half == 1 else 0)
        rows = pl.ds(pl.multiple_of(start, 16), S if half is None else 16)
        if q < 3:
            return LB.at[q, rows, :]
        if q < 5:
            return PB.at[0, core, 2 * (q - 3) : 2 * (q - 2), rows, :]
        if q == 5:
            return PB.at[2, :, d2, rows, :]
        return PB.at[1, core, 2 * (q - 6) : 2 * (q - 5), rows, :]

    def ring(q, way, t):
        owner = rem(y + (8 - t if way == 0 else t), 8)
        ref = block(q, owner, way if t == 3 else None)
        return pltpu.make_async_remote_copy(
            ref, ref, ring_s.at[q], ring_r.at[q, way, t],
            device_id=(r, right if way == 0 else left), device_id_type=MESH,
        )

    def arrival(q, way, t):
        owner = rem(y + (7 - t if way == 0 else t + 1), 8)
        ref = block(q, owner, way if t == 3 else None)
        return ref

    def to_sibling(ref, q):
        return pltpu.make_async_remote_copy(
            ref, ref, sib_s.at[q], sib_r.at[q], device_id=(sibling, y), device_id_type=MESH,
        )

    def ring_begin(q):
        for way in range(2):
            ring(q, way, 0).start()
        if q in SHARED:
            to_sibling(block(q, y, None), q).start()

    def ring_step(q, t):
        for way in range(2):
            ref = arrival(q, way, t)
            arrived(ref, ring_r.at[q, way, t])
            if t < 3:
                ring(q, way, t + 1).start()
            if q in SHARED:
                to_sibling(ref, q).start()

    for q in range(3):
        ring_begin(q)
    arrived(WS, ld.at[1])

    def pre0(level, side):
        to = level + 2 * side
        return pltpu.make_async_remote_copy(
            WS.at[level], PB.at[0, level, d0, mine, :], pg_s.at[0], pg_r.at[0],
            device_id=(row(jnp.int32(to), d1, d2), y), device_id_type=MESH,
        )

    def pre0_own(level):
        return pltpu.make_async_copy(WS.at[level], PB.at[0, level, d0, mine, :], pg_r.at[0])

    for level in range(2):
        for side in range(2):

            @pl.when(d0 != level + 2 * side)
            def _():
                pre0(level, side).start()

            @pl.when(d0 == level + 2 * side)
            def _():
                pre0_own(level).start()

    def pre1(level, side):
        return pltpu.make_async_remote_copy(
            WS.at[2 + level], PB.at[1, level, d1, mine, :], pg_s.at[1], pg_r.at[1],
            device_id=(row(level + 2 * z0, side + 2 * core, d2), y), device_id_type=MESH,
        )

    def pre1_own(level, side):
        return jnp.logical_and(self_a, jnp.logical_and(core == level, z1 == side))

    for level in range(2):
        for side in range(2):

            @pl.when(jnp.logical_not(pre1_own(level, side)))
            def _():
                pre1(level, side).start()

            @pl.when(pre1_own(level, side))
            def _():
                pltpu.make_async_copy(WS.at[2 + level], PB.at[1, level, d1, mine, :], pg_r.at[1]).start()

    own2 = pltpu.make_async_copy(WS.at[4:6], PB.at[2, :, d2, mine, :], pg_r.at[2])
    own2.start()

    for q in range(3):
        ring_step(q, 0)
    arrived(PB.at[0, core, :, mine, :], pg_r.at[0])
    ring_begin(3)
    for q in range(3):
        ring_step(q, 1)
    ring_begin(4)
    for q in range(3):
        ring_step(q, 2)
    ring_step(3, 0)
    for n in range(2):
        ring_step(n, 3)
        flat = LB[n]
        put(VT.at[n], flat)
        put(VN.at[n], jnp.transpose(flat))
    ring_step(2, 3)
    put(TT, triangle(LB[2]))
    ring_step(4, 0)
    own2.wait()

    def spread(k):
        other = 2 - 2 * z0
        return jnp.where(
            k == 0, other + core, jnp.where(k == 1, other + 1 - core, jnp.where(k == 2, 2 * z0 + 1 - core, d0))
        )

    def a_copy(h, k):
        to = spread(k)
        return pltpu.make_async_remote_copy(
            SND.at[to, h], X0.at[h, d0], top_s.at[0], top_r.at[0, h],
            device_id=(row(to, d1, d2), y), device_id_type=MESH,
        )

    def leaf(h):
        cols = slice(h * W, (h + 1) * W)
        quarters = [spread(k) for k in range(4)]
        if h == 0:
            arrived(A4, lda)
        inner = [mul(VT.at[0], A4[q, :B, cols]) + mul(VT.at[1], A4[q, B:, cols]) for q in quarters]
        scaled = [mul(TT, v) for v in inner]
        taken = [mul(VN.at[0], v) for v in scaled]
        for k, q in enumerate(quarters):
            SND[q, h] = A4[q, :B, cols] - taken[k]
            if k < 3:
                a_copy(h, k).start()
            else:
                pltpu.make_async_copy(SND.at[d0, h], X0.at[h, d0], top_r.at[0, h]).start()
        for k, q in enumerate(quarters):
            SC[q, h] = scaled[k]

    def remainder(h):
        cols = slice(h * W, (h + 1) * W)
        taken = [mul(VN.at[1], SC[c, h]) for c in range(4)]
        for c in range(4):
            out[B:, c * B + h * W : c * B + (h + 1) * W] = A4[c, B:, cols] - taken[c]

    leaf(0)
    ring_step(3, 1)
    leaf(1)
    ring_step(4, 1)
    ring_begin(5)
    ring_step(3, 2)
    remainder(0)
    ring_step(4, 2)
    arrived(PB.at[1, core, :, mine, :], pg_r.at[1])
    ring_begin(6)
    ring_step(3, 3)
    ring_step(4, 3)
    ring_step(5, 0)
    ring_begin(7)

    def sibling_wait(phase):
        for part in range(2):
            arrived(PB.at[phase, 1 - core, 2 * part : 2 * part + 2], sib_r.at[SHARED[2 * phase + part]])

    def prepare(q):
        for e in range(4):
            level, n = e // 2, e % 2
            k = (2 - level) * n
            p = k + 1 + level
            put(FT.at[e], triangle(PB[q, level, k]))
            turned = PB[q, level, p]
            put(YT.at[e], turned)
            put(YN.at[e], jnp.transpose(turned))

    def apply(X, h):
        tops = [X[h, i] for i in range(4)]
        for level in range(2):
            at = [((2 - level) * n, (2 - level) * n + 1 + level) for n in range(2)]
            summed = [tops[k] + mul(YT.at[2 * level + n], tops[p]) for n, (k, p) in enumerate(at)]
            coupling = [mul(FT.at[2 * level + n], v) for n, v in enumerate(summed)]
            taken = [mul(YN.at[2 * level + n], v) for n, v in enumerate(coupling)]
            for n, (k, p) in enumerate(at):
                tops[k] = tops[k] - coupling[n]
                tops[p] = tops[p] - taken[n]
        for i in range(4):
            X[h, i] = tops[i]

    kept_b = z2 + 2 * z0

    def b_copy(h, t):
        i = rem(kept_b + t, 4)
        return pltpu.make_async_remote_copy(
            X0.at[h, i], X1.at[h, d1], top_s.at[1], top_r.at[1, h],
            device_id=(row(core + 2 * div(i, 2), z0 + 2 * rem(i, 2), d2), y), device_id_type=MESH,
        )

    def c_copy(h, t):
        i = rem(d1 + t, 4)
        return pltpu.make_async_remote_copy(
            X1.at[h, i], X2.at[h, d2], top_s.at[2], top_r.at[2, h],
            device_id=(row(z2 + 2 * z0, i, rem(core + 2 * z1 + i, 4)), y), device_id_type=MESH,
        )

    def home(h):
        quarter = rem(d2 - d1 + 4, 4)
        return out.at[:B, pl.ds(pl.multiple_of(quarter * B + h * W, W), W)]

    def f_copy(h, t):
        i = rem(d2 + t, 4)
        return pltpu.make_async_remote_copy(
            X2.at[h, i], home(h), top_s.at[3], top_r.at[3, h],
            device_id=(row(d0, d1, i), y), device_id_type=MESH,
        )

    def send(copy, h, own, local):
        for t in (2, 1, 3):
            copy(h, t).start()
        if own is None:
            local().start()
        else:

            @pl.when(jnp.logical_not(own))
            def _():
                copy(h, 0).start()

            @pl.when(own)
            def _():
                local().start()

    def late(t):
        return pltpu.make_async_remote_copy(
            PB.at[2, :, d2], PB.at[2, :, d2], late_s, late_r,
            device_id=(row(d0, d1, rem(d2 + t, 4)), y), device_id_type=MESH,
        )

    sibling_wait(0)
    prepare(0)
    for h in range(2):
        arrived(X0.at[h], top_r.at[0, h])
        apply(X0, h)
        send(b_copy, h, self_b, lambda: pltpu.make_async_copy(X0.at[h, kept_b], X1.at[h, d1], top_r.at[1, h]))
        if h == 0:
            ring_step(5, 1)
            ring_step(6, 0)
    ring_step(5, 2)
    ring_step(7, 0)
    ring_step(5, 3)
    for t in (2, 1, 3):
        late(t).start()
    ring_step(6, 1)
    ring_step(7, 1)
    remainder(1)
    ring_step(6, 2)
    ring_step(7, 2)
    ring_step(6, 3)
    ring_step(7, 3)
    sibling_wait(1)
    prepare(1)


    for h in range(2):
        arrived(X1.at[h], top_r.at[1, h])
        apply(X1, h)
        send(c_copy, h, self_c, lambda: pltpu.make_async_copy(X1.at[h, d1], X2.at[h, d2], top_r.at[2, h]))

    arrived(PB.at[2, :, 0:3], late_r)
    prepare(2)

    for h in range(2):
        arrived(X2.at[h], top_r.at[2, h])
        apply(X2, h)
        send(f_copy, h, None, lambda: pltpu.make_async_copy(X2.at[h, d2], home(h), top_r.at[3, h]))

    for h in range(2):
        arrived(out.at[:B, 0 : 4 * W], top_r.at[3, h])

    for q in range(8):
        rows = pl.ds(0, 7 * S)
        arrived(LB.at[q, rows] if q < 3 else PB.at[0, 0, 0:2, rows], ring_s.at[q])
    for q in SHARED:
        arrived(PB.at[0, 0, 0:2], sib_s.at[q])
    arrived(WS.at[0:3], pg_s.at[0])
    arrived(PB.at[2, :, 0:3], late_s)
    arrived(X0.at[:, 0:3], top_s.at[0])
    arrived(X0.at[:, 0:3], top_s.at[3])
    for own, sem, few, all_ in (
        (self_a, pg_s.at[1], WS.at[0:3], WS.at[0:4]),
        (self_b, top_s.at[1], X0.at[:, 0:3], X0),
        (self_c, top_s.at[2], X1.at[:, 0:3], X1),
    ):

        @pl.when(own)
        def _():
            arrived(few, sem)

        @pl.when(jnp.logical_not(own))
        def _():
            arrived(all_, sem)


def per_device(trailing, reflectors, leaf_factor, node_reflect, node_factor):
    anywhere = pl.BlockSpec(memory_space=pl.ANY)
    dma = pltpu.SemaphoreType.DMA
    tops = pltpu.VMEM((2, 4, B, W), F32)
    nodes = pltpu.VMEM((4, 2 * B, B), BF16)
    return pl.pallas_call(
        kernel,
        out_shape=pltpu.VMEM(trailing.shape, F32),
        in_specs=[anywhere] * 5,
        out_specs=pl.BlockSpec(memory_space=pltpu.VMEM),
        scratch_shapes=[
            pltpu.VMEM((6, S, B), F32),
            pltpu.VMEM((3, B, B), F32),
            pltpu.VMEM((3, 2, 4, B, B), F32),
            pltpu.VMEM((4, 2 * B, B), F32),
            pltpu.VMEM((4, 2, B, W), F32),
            pltpu.VMEM((4, 2, B, W), F32),
            tops, tops, tops,
            pltpu.VMEM((2, 2 * B, B), BF16),
            pltpu.VMEM((2, 2 * B, B), BF16),
            pltpu.VMEM((2 * B, B), BF16),
            nodes, nodes, nodes,
            dma((2,)), dma,
            dma((8,)), dma((8, 2, 4)),
            dma((2,)), dma((3,)),
            dma((8,)), dma((8,)),
            dma, dma,
            dma((4,)), dma((4, 2)),
        ],
        compiler_params=pltpu.CompilerParams(
            collective_id=0, has_side_effects=True, vmem_limit_bytes=56 * 1024 * 1024
        ),
        name="update",
    )(
        trailing,
        reflectors.T,
        leaf_factor.T,
        jnp.swapaxes(node_reflect, 1, 2),
        jnp.swapaxes(node_factor, 1, 2),
    )


def solution(mesh):
    in_specs = (
        P("row", "col"),
        P("row", "col"),
        P("row", "col"),
        P(None, "row", "col"),
        P(None, "row", "col"),
    )
    return jax.shard_map(
        per_device, mesh=mesh, in_specs=in_specs, out_specs=P("row", "col"), check_vma=False
    )
```

```python
import jax
import jax.numpy as jnp
from jax import lax
from jax.experimental import pallas as pl
from jax.experimental.pallas import tpu as pltpu
from jax.sharding import PartitionSpec as P

B = 256
S = 32
W = 128
SHARED = (3, 4, 6, 7, 5)
MESH = pl.DeviceIdType.MESH
F32 = jnp.float32
BF16 = jnp.bfloat16


def rem(a, b):
    return lax.rem(a, jnp.int32(b))


def div(a, b):
    return lax.div(a, jnp.int32(b))


def split(x):
    hi = x.astype(BF16)
    lo = (x - hi.astype(F32)).astype(BF16)
    return hi, lo


def dot(a, b):
    return jnp.dot(a, b, preferred_element_type=F32)


def mul(stacked, x):
    both = dot(stacked[...], jnp.concatenate(split(x), axis=1))
    return both[:B, :W] + (both[:B, W:] + both[B:, :W])


def put(stacked, x):
    hi, lo = split(x)
    stacked[:B] = hi
    stacked[B:] = lo


def triangle(turned):
    row = lax.broadcasted_iota(jnp.int32, (B, B), 0)
    col = lax.broadcasted_iota(jnp.int32, (B, B), 1)
    kept = jnp.where(col <= row, turned, 0.0)
    return kept + jnp.where(col == row, 0.5, 0.0).astype(F32)


def kernel(
    tr, vh, th, nr, nf, out,
    WS, LB, PB, A4, SND, SC, X0, X1, X2,
    VT, VN, TT, FT, YT, YN,
    ld, lda, ring_s, ring_r, pg_s, pg_r, sib_s, sib_r, top_s, top_r,
):
    r = lax.axis_index("row")
    y = lax.axis_index("col")
    d0 = rem(r, 4)
    d1 = rem(div(r, 4), 4)
    d2 = div(r, 16)
    core = rem(d0, 2)
    z0 = div(d0, 2)
    z1 = rem(d1, 2)
    z2 = div(d1, 2)
    x0 = rem(d2, 2)
    x1 = div(d2, 2)
    group = rem(x0 + z1, 2)
    flip = rem(x1 + z2, 2)
    turn = rem(core + z1, 2)

    def row(a, b, c):
        return a + 4 * b + 16 * c

    right = rem(y + 1, 8)
    left = rem(y + 7, 8)
    sibling = row(d0 + 1 - 2 * core, d1, d2)

    mine = pl.ds(pl.multiple_of(y * S, S), S)

    pltpu.make_async_copy(vh.at[:, :B], LB.at[0, mine, :], ld.at[0]).start()
    pltpu.make_async_copy(vh.at[:, B:], LB.at[1, mine, :], ld.at[0]).start()
    pltpu.make_async_copy(th, LB.at[2, mine, :], ld.at[0]).start()
    bits = [rem(div(r, 1 << s), 2) for s in range(6)]
    for s in range(6):

        @pl.when(bits[s] == 0)
        def _():
            pltpu.make_async_copy(nf.at[s], WS.at[s], ld.at[1]).start()

        @pl.when(bits[s] == 1)
        def _():
            pltpu.make_async_copy(nr.at[s], WS.at[s], ld.at[1]).start()

    for c in range(4):
        pltpu.make_async_copy(tr.at[:, c * B : (c + 1) * B], A4.at[c], lda).start()

    barrier = pltpu.get_barrier_semaphore()

    def greet(a, b):
        pl.semaphore_signal(barrier, inc=1, device_id=(a, b), device_id_type=MESH)

    greet(r, right)
    greet(r, left)
    for t in range(1, 4):
        greet(row(rem(d0 + t, 4), d1, d2), y)
    self_a = z2 == core
    self_b = z1 == z0
    self_c = d2 == 3 * rem(z1 + z2, 2)
    self_d = group == core
    for t in range(4):
        back_d0 = rem(core + t, 2) + 2 * z0
        back_d2 = turn + 2 * rem(x1 + t // 2, 2)
        sources = (
            (self_a, row(z2 + 2 * z0, rem(d1 + t, 4), d2)),
            (self_b, row(core + 2 * z1, rem(d1 + t, 4), d2)),
            (self_c, row(d0, flip + 2 * group, rem(d2 + t, 4))),
            (self_d, row(group + 2 * z0, d1, rem(d2 + t, 4))),
            (self_d, row(back_d0, d1, back_d2)),
        )
        for own, source in sources:
            if t:
                greet(source, y)
            else:

                @pl.when(jnp.logical_not(own))
                def _():
                    greet(source, y)

    def arrived(ref, sem):
        pltpu.make_async_copy(ref, ref, sem).wait()

    arrived(LB.at[:, mine, :], ld.at[0])
    expected = 5 + 15
    for own in (self_a, self_b, self_c, self_d, self_d):
        expected = expected + jnp.where(own, 0, 1)
    pl.semaphore_wait(barrier, expected)

    def block(q, owner, half):
        start = owner * S + (16 if half == 1 else 0)
        rows = pl.ds(pl.multiple_of(start, 16), S if half is None else 16)
        if q < 3:
            return LB.at[q, rows, :]
        if q < 5:
            return PB.at[0, core, 2 * (q - 3) : 2 * (q - 2), rows, :]
        if q == 5:
            return PB.at[2, core, :, rows, :]
        return PB.at[1, core, 2 * (q - 6) : 2 * (q - 5), rows, :]

    def ring(q, way, t):
        owner = rem(y + (8 - t if way == 0 else t), 8)
        ref = block(q, owner, way if t == 3 else None)
        return pltpu.make_async_remote_copy(
            ref, ref, ring_s.at[q], ring_r.at[q, way, t],
            device_id=(r, right if way == 0 else left), device_id_type=MESH,
        )

    def arrival(q, way, t):
        owner = rem(y + (7 - t if way == 0 else t + 1), 8)
        ref = block(q, owner, way if t == 3 else None)
        return ref

    def to_sibling(ref, q):
        return pltpu.make_async_remote_copy(
            ref, ref, sib_s.at[q], sib_r.at[q], device_id=(sibling, y), device_id_type=MESH,
        )

    def ring_begin(q):
        for way in range(2):
            ring(q, way, 0).start()
        if q in SHARED:
            to_sibling(block(q, y, None), q).start()

    def ring_step(q, t):
        for way in range(2):
            ref = arrival(q, way, t)
            arrived(ref, ring_r.at[q, way, t])
            if t < 3:
                ring(q, way, t + 1).start()
            if q in SHARED:
                to_sibling(ref, q).start()

    for q in range(3):
        ring_begin(q)
    arrived(WS, ld.at[1])

    def pre0(level, side):
        to = level + 2 * side
        return pltpu.make_async_remote_copy(
            WS.at[level], PB.at[0, level, d0, mine, :], pg_s.at[0], pg_r.at[0],
            device_id=(row(jnp.int32(to), d1, d2), y), device_id_type=MESH,
        )

    def pre0_own(level):
        return pltpu.make_async_copy(WS.at[level], PB.at[0, level, d0, mine, :], pg_r.at[0])

    for level in range(2):
        for side in range(2):

            @pl.when(d0 != level + 2 * side)
            def _():
                pre0(level, side).start()

            @pl.when(d0 == level + 2 * side)
            def _():
                pre0_own(level).start()

    def pre1(level, side):
        return pltpu.make_async_remote_copy(
            WS.at[2 + level], PB.at[1, level, d1, mine, :], pg_s.at[1], pg_r.at[1],
            device_id=(row(level + 2 * z0, side + 2 * core, d2), y), device_id_type=MESH,
        )

    def pre1_own(level, side):
        return jnp.logical_and(self_a, jnp.logical_and(core == level, z1 == side))

    for level in range(2):
        for side in range(2):

            @pl.when(jnp.logical_not(pre1_own(level, side)))
            def _():
                pre1(level, side).start()

            @pl.when(pre1_own(level, side))
            def _():
                pltpu.make_async_copy(WS.at[2 + level], PB.at[1, level, d1, mine, :], pg_r.at[1]).start()

    def pre2(level, side):
        return pltpu.make_async_remote_copy(
            WS.at[4 + level], PB.at[2, level, d2, mine, :], pg_s.at[2], pg_r.at[2],
            device_id=(row(level + 2 * z0, d1, turn + 2 * side), y), device_id_type=MESH,
        )

    def pre2_own(level, side):
        return jnp.logical_and(self_d, jnp.logical_and(core == level, x1 == side))

    for level in range(2):
        for side in range(2):

            @pl.when(jnp.logical_not(pre2_own(level, side)))
            def _():
                pre2(level, side).start()

            @pl.when(pre2_own(level, side))
            def _():
                pltpu.make_async_copy(WS.at[4 + level], PB.at[2, level, d2, mine, :], pg_r.at[2]).start()

    for q in range(3):
        ring_step(q, 0)
    arrived(PB.at[0, core, :, mine, :], pg_r.at[0])
    ring_begin(3)
    ring_begin(4)
    for q in range(3):
        ring_step(q, 1)
    ring_step(3, 0)
    ring_step(4, 0)
    for q in range(3):
        ring_step(q, 2)
    ring_step(3, 1)
    for n in range(2):
        ring_step(n, 3)
        flat = LB[n]
        put(VT.at[n], flat)
        put(VN.at[n], jnp.transpose(flat))
    ring_step(2, 3)
    put(TT, triangle(LB[2]))
    ring_step(4, 1)

    def spread(k):
        other = 2 - 2 * z0
        return jnp.where(
            k == 0, other + core, jnp.where(k == 1, other + 1 - core, jnp.where(k == 2, 2 * z0 + 1 - core, d0))
        )

    def a_copy(h, k):
        to = spread(k)
        return pltpu.make_async_remote_copy(
            SND.at[to, h], X0.at[h, d0], top_s.at[0], top_r.at[0, h],
            device_id=(row(to, d1, d2), y), device_id_type=MESH,
        )

    def leaf(h):
        cols = slice(h * W, (h + 1) * W)
        quarters = [spread(k) for k in range(4)]
        if h == 0:
            arrived(A4, lda)
        inner = [mul(VT.at[0], A4[q, :B, cols]) + mul(VT.at[1], A4[q, B:, cols]) for q in quarters]
        scaled = [mul(TT, v) for v in inner]
        taken = [mul(VN.at[0], v) for v in scaled]
        for k, q in enumerate(quarters):
            SND[q, h] = A4[q, :B, cols] - taken[k]
            if k < 3:
                a_copy(h, k).start()
            else:
                pltpu.make_async_copy(SND.at[d0, h], X0.at[h, d0], top_r.at[0, h]).start()
        for k, q in enumerate(quarters):
            SC[q, h] = scaled[k]

    def remainder(h):
        cols = slice(h * W, (h + 1) * W)
        taken = [mul(VN.at[1], SC[c, h]) for c in range(4)]
        for c in range(4):
            out[B:, c * B + h * W : c * B + (h + 1) * W] = A4[c, B:, cols] - taken[c]

    leaf(0)
    ring_step(3, 2)
    leaf(1)
    ring_step(4, 2)
    arrived(PB.at[1, core, :, mine, :], pg_r.at[1])
    ring_begin(6)
    ring_step(3, 3)
    ring_step(4, 3)
    ring_begin(7)
    ring_step(6, 0)

    def sibling_wait(phase):
        if phase == 2:
            arrived(PB.at[2, 1 - core], sib_r.at[5])
        else:
            for part in range(2):
                arrived(PB.at[phase, 1 - core, 2 * part : 2 * part + 2], sib_r.at[SHARED[2 * phase + part]])

    def prepare(q):
        for e in range(4):
            level, n = e // 2, e % 2
            k = (2 - level) * n
            p = k + 1 + level
            put(FT.at[e], triangle(PB[q, level, k]))
            turned = PB[q, level, p]
            put(YN.at[e], jnp.transpose(turned))
            if q == 0:
                put(YT.at[e], turned)
            else:
                for c in range(2):
                    cols = slice(c * W, (c + 1) * W)
                    hi, lo = split(mul(FT.at[e], turned[:, cols]))
                    YT[e, :B, cols] = hi
                    YT[e, B:, cols] = lo

    def apply(X, h):
        tops = [X[h, i] for i in range(4)]
        for level in range(2):
            at = [((2 - level) * n, (2 - level) * n + 1 + level) for n in range(2)]
            if X is X0:
                summed = [tops[k] + mul(YT.at[2 * level + n], tops[p]) for n, (k, p) in enumerate(at)]
                coupling = [mul(FT.at[2 * level + n], v) for n, v in enumerate(summed)]
            else:
                coupling = [
                    mul(FT.at[2 * level + n], tops[k]) + mul(YT.at[2 * level + n], tops[p])
                    for n, (k, p) in enumerate(at)
                ]
            taken = [mul(YN.at[2 * level + n], v) for n, v in enumerate(coupling)]
            for n, (k, p) in enumerate(at):
                tops[k] = tops[k] - coupling[n]
                tops[p] = tops[p] - taken[n]
        for i in range(4):
            X[h, i] = tops[i]

    kept_b = z2 + 2 * z0

    def b_copy(h, t):
        i = rem(kept_b + t, 4)
        return pltpu.make_async_remote_copy(
            X0.at[h, i], X1.at[h, d1], top_s.at[1], top_r.at[1, h],
            device_id=(row(core + 2 * div(i, 2), z0 + 2 * rem(i, 2), d2), y), device_id_type=MESH,
        )

    def c_copy(h, t):
        i = rem(d1 + t, 4)
        return pltpu.make_async_remote_copy(
            X1.at[h, i], X2.at[h, d2], top_s.at[2], top_r.at[2, h],
            device_id=(row(d0, i, rem(z2 + i, 2) + 2 * rem(z1 + div(i, 2), 2)), y), device_id_type=MESH,
        )

    def home(h):
        quarter = core + 2 * flip
        return out.at[:B, pl.ds(pl.multiple_of(quarter * B + h * W, W), W)]

    def f_copy(h, t):
        i = rem(d2 + t, 4)
        return pltpu.make_async_remote_copy(
            X2.at[h, i], home(h), top_s.at[3], top_r.at[3, h],
            device_id=(row(group + 2 * z0, d1, i), y), device_id_type=MESH,
        )

    def send(copy, h, own, local):
        for t in (2, 1, 3):
            copy(h, t).start()

        @pl.when(jnp.logical_not(own))
        def _():
            copy(h, 0).start()

        @pl.when(own)
        def _():
            local().start()

    sibling_wait(0)
    prepare(0)
    for h in range(2):
        arrived(X0.at[h], top_r.at[0, h])
        apply(X0, h)
        send(b_copy, h, self_b, lambda: pltpu.make_async_copy(X0.at[h, kept_b], X1.at[h, d1], top_r.at[1, h]))
        if h == 0:
            ring_step(7, 0)
    ring_step(6, 1)
    ring_step(7, 1)
    arrived(PB.at[2, core, :, mine, :], pg_r.at[2])
    ring_step(6, 2)
    ring_step(7, 2)
    ring_begin(5)
    ring_step(6, 3)
    remainder(0)
    ring_step(7, 3)
    ring_step(5, 0)
    sibling_wait(1)
    prepare(1)


    ring_step(5, 1)
    for h in range(2):
        arrived(X1.at[h], top_r.at[1, h])
        apply(X1, h)
        send(c_copy, h, self_c, lambda: pltpu.make_async_copy(X1.at[h, d1], X2.at[h, d2], top_r.at[2, h]))
        if h == 0:
            for t in range(2, 4):
                ring_step(5, t)
            remainder(1)
    sibling_wait(2)
    prepare(2)

    for h in range(2):
        arrived(X2.at[h], top_r.at[2, h])
        apply(X2, h)
        send(f_copy, h, self_d, lambda: pltpu.make_async_copy(X2.at[h, d2], home(h), top_r.at[3, h]))

    for h in range(2):
        arrived(out.at[:B, 0 : 4 * W], top_r.at[3, h])

    for q in range(8):
        rows = pl.ds(0, 7 * S)
        arrived(LB.at[q, rows] if q < 3 else PB.at[0, 0, 0 : 4 if q == 5 else 2, rows], ring_s.at[q])
    for q in SHARED:
        arrived(PB.at[0, 0, 0 : 4 if q == 5 else 2], sib_s.at[q])
    arrived(WS.at[0:3], pg_s.at[0])
    arrived(X0.at[:, 0:3], top_s.at[0])
    for own, sem, few, all_ in (
        (self_a, pg_s.at[1], WS.at[0:3], WS.at[0:4]),
        (self_b, top_s.at[1], X0.at[:, 0:3], X0),
        (self_c, top_s.at[2], X1.at[:, 0:3], X1),
        (self_d, pg_s.at[2], WS.at[0:3], WS.at[0:4]),
        (self_d, top_s.at[3], X2.at[:, 0:3], X2),
    ):

        @pl.when(own)
        def _():
            arrived(few, sem)

        @pl.when(jnp.logical_not(own))
        def _():
            arrived(all_, sem)


def per_device(trailing, reflectors, leaf_factor, node_reflect, node_factor):
    anywhere = pl.BlockSpec(memory_space=pl.ANY)
    dma = pltpu.SemaphoreType.DMA
    tops = pltpu.VMEM((2, 4, B, W), F32)
    nodes = pltpu.VMEM((4, 2 * B, B), BF16)
    return pl.pallas_call(
        kernel,
        out_shape=pltpu.VMEM(trailing.shape, F32),
        in_specs=[anywhere] * 5,
        out_specs=pl.BlockSpec(memory_space=pltpu.VMEM),
        scratch_shapes=[
            pltpu.VMEM((6, S, B), F32),
            pltpu.VMEM((3, B, B), F32),
            pltpu.VMEM((3, 2, 4, B, B), F32),
            pltpu.VMEM((4, 2 * B, B), F32),
            pltpu.VMEM((4, 2, B, W), F32),
            pltpu.VMEM((4, 2, B, W), F32),
            tops, tops, tops,
            pltpu.VMEM((2, 2 * B, B), BF16),
            pltpu.VMEM((2, 2 * B, B), BF16),
            pltpu.VMEM((2 * B, B), BF16),
            nodes, nodes, nodes,
            dma((2,)), dma,
            dma((8,)), dma((8, 2, 4)),
            dma((3,)), dma((3,)),
            dma((8,)), dma((8,)),
            dma((4,)), dma((4, 2)),
        ],
        compiler_params=pltpu.CompilerParams(
            collective_id=0, has_side_effects=True, vmem_limit_bytes=56 * 1024 * 1024
        ),
        name="update",
    )(
        trailing,
        reflectors.T,
        leaf_factor.T,
        jnp.swapaxes(node_reflect, 1, 2),
        jnp.swapaxes(node_factor, 1, 2),
    )


def solution(mesh):
    in_specs = (
        P("row", "col"),
        P("row", "col"),
        P("row", "col"),
        P(None, "row", "col"),
        P(None, "row", "col"),
    )
    return jax.shard_map(
        per_device, mesh=mesh, in_specs=in_specs, out_specs=P("row", "col"), check_vma=False
    )
```

```python
import jax
import jax.numpy as jnp
from jax import lax
from jax.experimental import pallas as pl
from jax.experimental.pallas import tpu as pltpu
from jax.sharding import PartitionSpec as P

B = 256
S = 32
W = 128
SHARED = (3, 4, 6, 7, 5)
MESH = pl.DeviceIdType.MESH
F32 = jnp.float32
BF16 = jnp.bfloat16


def rem(a, b):
    return lax.rem(a, jnp.int32(b))


def div(a, b):
    return lax.div(a, jnp.int32(b))


def split(x):
    hi = x.astype(BF16)
    lo = (x - hi.astype(F32)).astype(BF16)
    return hi, lo


def dot(a, b):
    return jnp.dot(a, b, preferred_element_type=F32)


def mul(stacked, x):
    both = dot(stacked[...], jnp.concatenate(split(x), axis=1))
    return both[:B, :W] + (both[:B, W:] + both[B:, :W])


def put(stacked, x):
    hi, lo = split(x)
    stacked[:B] = hi
    stacked[B:] = lo


def triangle(turned):
    row = lax.broadcasted_iota(jnp.int32, (B, B), 0)
    col = lax.broadcasted_iota(jnp.int32, (B, B), 1)
    kept = jnp.where(col <= row, turned, 0.0)
    return kept + jnp.where(col == row, 0.5, 0.0).astype(F32)


def kernel(
    tr, vh, th, nr, nf, out,
    WS, LB, PB, A4, SND, SC, X0, X1, X2,
    VT, VN, TT, FT, YT, YN,
    ld, lda, ring_s, ring_r, pg_s, pg_r, sib_s, sib_r, top_s, top_r,
):
    r = lax.axis_index("row")
    y = lax.axis_index("col")
    d0 = rem(r, 4)
    d1 = rem(div(r, 4), 4)
    d2 = div(r, 16)
    core = rem(d0, 2)
    z0 = div(d0, 2)
    z1 = rem(d1, 2)
    z2 = div(d1, 2)
    x0 = rem(d2, 2)
    x1 = div(d2, 2)
    group = rem(x0 + z1, 2)
    flip = rem(x1 + z2, 2)
    turn = rem(core + z1, 2)

    def row(a, b, c):
        return a + 4 * b + 16 * c

    right = rem(y + 1, 8)
    left = rem(y + 7, 8)
    sibling = row(d0 + 1 - 2 * core, d1, d2)

    mine = pl.ds(pl.multiple_of(y * S, S), S)

    pltpu.make_async_copy(vh.at[:, :B], LB.at[0, mine, :], ld.at[0]).start()
    pltpu.make_async_copy(vh.at[:, B:], LB.at[1, mine, :], ld.at[0]).start()
    pltpu.make_async_copy(th, LB.at[2, mine, :], ld.at[0]).start()
    bits = [rem(div(r, 1 << s), 2) for s in range(6)]
    for s in range(6):

        @pl.when(bits[s] == 0)
        def _():
            pltpu.make_async_copy(nf.at[s], WS.at[s], ld.at[1]).start()

        @pl.when(bits[s] == 1)
        def _():
            pltpu.make_async_copy(nr.at[s], WS.at[s], ld.at[1]).start()

    for c in range(4):
        pltpu.make_async_copy(tr.at[:, c * B : (c + 1) * B], A4.at[c], lda).start()

    barrier = pltpu.get_barrier_semaphore()

    def greet(a, b):
        pl.semaphore_signal(barrier, inc=1, device_id=(a, b), device_id_type=MESH)

    greet(r, right)
    greet(r, left)
    for t in range(1, 4):
        greet(row(rem(d0 + t, 4), d1, d2), y)
    self_a = z2 == core
    self_b = z1 == z0
    self_c = d2 == 3 * rem(z1 + z2, 2)
    self_d = group == core
    for t in range(4):
        back_d0 = rem(core + t, 2) + 2 * z0
        back_d2 = turn + 2 * rem(x1 + t // 2, 2)
        sources = (
            (self_a, row(z2 + 2 * z0, rem(d1 + t, 4), d2)),
            (self_b, row(core + 2 * z1, rem(d1 + t, 4), d2)),
            (self_c, row(d0, flip + 2 * group, rem(d2 + t, 4))),
            (self_d, row(group + 2 * z0, d1, rem(d2 + t, 4))),
            (self_d, row(back_d0, d1, back_d2)),
        )
        for own, source in sources:
            if t:
                greet(source, y)
            else:

                @pl.when(jnp.logical_not(own))
                def _():
                    greet(source, y)

    def arrived(ref, sem):
        pltpu.make_async_copy(ref, ref, sem).wait()

    arrived(LB.at[:, mine, :], ld.at[0])
    expected = 5 + 15
    for own in (self_a, self_b, self_c, self_d, self_d):
        expected = expected + jnp.where(own, 0, 1)
    pl.semaphore_wait(barrier, expected)

    def block(q, owner, half):
        start = owner * S + (16 if half == 1 else 0)
        rows = pl.ds(pl.multiple_of(start, 16), S if half is None else 16)
        if q < 3:
            return LB.at[q, rows, :]
        if q < 5:
            return PB.at[0, core, 2 * (q - 3) : 2 * (q - 2), rows, :]
        if q == 5:
            return PB.at[2, core, :, rows, :]
        return PB.at[1, core, 2 * (q - 6) : 2 * (q - 5), rows, :]

    def ring(q, way, t):
        owner = rem(y + (8 - t if way == 0 else t), 8)
        ref = block(q, owner, way if t == 3 else None)
        return pltpu.make_async_remote_copy(
            ref, ref, ring_s.at[q], ring_r.at[q, way, t],
            device_id=(r, right if way == 0 else left), device_id_type=MESH,
        )

    def arrival(q, way, t):
        owner = rem(y + (7 - t if way == 0 else t + 1), 8)
        ref = block(q, owner, way if t == 3 else None)
        return ref

    def to_sibling(ref, q):
        return pltpu.make_async_remote_copy(
            ref, ref, sib_s.at[q], sib_r.at[q], device_id=(sibling, y), device_id_type=MESH,
        )

    def ring_begin(q):
        for way in range(2):
            ring(q, way, 0).start()
        if q in SHARED:
            to_sibling(block(q, y, None), q).start()

    def ring_step(q, t):
        for way in range(2):
            ref = arrival(q, way, t)
            arrived(ref, ring_r.at[q, way, t])
            if t < 3:
                ring(q, way, t + 1).start()
            if q in SHARED:
                to_sibling(ref, q).start()

    for q in range(3):
        ring_begin(q)
    arrived(WS, ld.at[1])

    def pre0(level, side):
        to = level + 2 * side
        return pltpu.make_async_remote_copy(
            WS.at[level], PB.at[0, level, d0, mine, :], pg_s.at[0], pg_r.at[0],
            device_id=(row(jnp.int32(to), d1, d2), y), device_id_type=MESH,
        )

    def pre0_own(level):
        return pltpu.make_async_copy(WS.at[level], PB.at[0, level, d0, mine, :], pg_r.at[0])

    for level in range(2):
        for side in range(2):

            @pl.when(d0 != level + 2 * side)
            def _():
                pre0(level, side).start()

            @pl.when(d0 == level + 2 * side)
            def _():
                pre0_own(level).start()

    def pre1(level, side):
        return pltpu.make_async_remote_copy(
            WS.at[2 + level], PB.at[1, level, d1, mine, :], pg_s.at[1], pg_r.at[1],
            device_id=(row(level + 2 * z0, side + 2 * core, d2), y), device_id_type=MESH,
        )

    def pre1_own(level, side):
        return jnp.logical_and(self_a, jnp.logical_and(core == level, z1 == side))

    for level in range(2):
        for side in range(2):

            @pl.when(jnp.logical_not(pre1_own(level, side)))
            def _():
                pre1(level, side).start()

            @pl.when(pre1_own(level, side))
            def _():
                pltpu.make_async_copy(WS.at[2 + level], PB.at[1, level, d1, mine, :], pg_r.at[1]).start()

    def pre2(level, side):
        return pltpu.make_async_remote_copy(
            WS.at[4 + level], PB.at[2, level, d2, mine, :], pg_s.at[2], pg_r.at[2],
            device_id=(row(level + 2 * z0, d1, turn + 2 * side), y), device_id_type=MESH,
        )

    def pre2_own(level, side):
        return jnp.logical_and(self_d, jnp.logical_and(core == level, x1 == side))

    for level in range(2):
        for side in range(2):

            @pl.when(jnp.logical_not(pre2_own(level, side)))
            def _():
                pre2(level, side).start()

            @pl.when(pre2_own(level, side))
            def _():
                pltpu.make_async_copy(WS.at[4 + level], PB.at[2, level, d2, mine, :], pg_r.at[2]).start()

    for q in range(3):
        ring_step(q, 0)
    arrived(PB.at[0, core, :, mine, :], pg_r.at[0])
    ring_begin(3)
    ring_begin(4)
    for q in range(3):
        ring_step(q, 1)
    ring_step(3, 0)
    ring_step(4, 0)
    for q in range(3):
        ring_step(q, 2)
    ring_step(3, 1)
    for n in range(2):
        ring_step(n, 3)
        flat = LB[n]
        put(VT.at[n], flat)
        put(VN.at[n], jnp.transpose(flat))
    ring_step(2, 3)
    put(TT, triangle(LB[2]))
    ring_step(4, 1)

    def spread(k):
        other = 2 - 2 * z0
        return jnp.where(
            k == 0, other + core, jnp.where(k == 1, other + 1 - core, jnp.where(k == 2, 2 * z0 + 1 - core, d0))
        )

    def a_copy(h, k):
        to = spread(k)
        return pltpu.make_async_remote_copy(
            SND.at[to, h], X0.at[h, d0], top_s.at[0], top_r.at[0, h],
            device_id=(row(to, d1, d2), y), device_id_type=MESH,
        )

    def leaf(h):
        cols = slice(h * W, (h + 1) * W)
        quarters = [spread(k) for k in range(4)]
        if h == 0:
            arrived(A4, lda)
        inner = [mul(VT.at[0], A4[q, :B, cols]) + mul(VT.at[1], A4[q, B:, cols]) for q in quarters]
        scaled = [mul(TT, v) for v in inner]
        taken = [mul(VN.at[0], v) for v in scaled]
        for k, q in enumerate(quarters):
            SND[q, h] = A4[q, :B, cols] - taken[k]
            if k < 3:
                a_copy(h, k).start()
            else:
                pltpu.make_async_copy(SND.at[d0, h], X0.at[h, d0], top_r.at[0, h]).start()
        for k, q in enumerate(quarters):
            SC[q, h] = scaled[k]

    def remainder(h):
        cols = slice(h * W, (h + 1) * W)
        taken = [mul(VN.at[1], SC[c, h]) for c in range(4)]
        for c in range(4):
            out[B:, c * B + h * W : c * B + (h + 1) * W] = A4[c, B:, cols] - taken[c]

    leaf(0)
    ring_step(3, 2)
    leaf(1)
    ring_step(4, 2)
    arrived(PB.at[1, core, :, mine, :], pg_r.at[1])
    ring_begin(6)
    ring_step(3, 3)
    ring_step(4, 3)
    ring_begin(7)
    ring_step(6, 0)

    def sibling_wait(phase):
        if phase == 2:
            arrived(PB.at[2, 1 - core], sib_r.at[5])
        else:
            for part in range(2):
                arrived(PB.at[phase, 1 - core, 2 * part : 2 * part + 2], sib_r.at[SHARED[2 * phase + part]])

    def prepare_first(level):
        for n in range(2):
            k = (2 - level) * n
            e = 2 * level + n
            turned = PB[0, level, k + 1 + level]
            put(FT.at[e], triangle(PB[0, level, k]))
            put(YT.at[e], turned)
            put(YN.at[e], jnp.transpose(turned))

    def prepare(q):
        for e in range(4):
            level, n = e // 2, e % 2
            k = (2 - level) * n
            p = k + 1 + level
            put(FT.at[e], triangle(PB[q, level, k]))
            turned = PB[q, level, p]
            put(YN.at[e], jnp.transpose(turned))
            for c in range(2):
                cols = slice(c * W, (c + 1) * W)
                hi, lo = split(mul(FT.at[e], turned[:, cols]))
                YT[e, :B, cols] = hi
                YT[e, B:, cols] = lo

    def apply(X, h):
        tops = [X[h, i] for i in range(4)]
        for level in range(2):
            at = [((2 - level) * n, (2 - level) * n + 1 + level) for n in range(2)]
            if X is X0:
                summed = [tops[k] + mul(YT.at[2 * level + n], tops[p]) for n, (k, p) in enumerate(at)]
                coupling = [mul(FT.at[2 * level + n], v) for n, v in enumerate(summed)]
            else:
                coupling = [
                    mul(FT.at[2 * level + n], tops[k]) + mul(YT.at[2 * level + n], tops[p])
                    for n, (k, p) in enumerate(at)
                ]
            taken = [mul(YN.at[2 * level + n], v) for n, v in enumerate(coupling)]
            for n, (k, p) in enumerate(at):
                tops[k] = tops[k] - coupling[n]
                tops[p] = tops[p] - taken[n]
        for i in range(4):
            X[h, i] = tops[i]

    kept_b = z2 + 2 * z0

    def b_copy(h, t):
        i = rem(kept_b + t, 4)
        return pltpu.make_async_remote_copy(
            X0.at[h, i], X1.at[h, d1], top_s.at[1], top_r.at[1, h],
            device_id=(row(core + 2 * div(i, 2), z0 + 2 * rem(i, 2), d2), y), device_id_type=MESH,
        )

    def c_copy(h, t):
        i = rem(d1 + t, 4)
        return pltpu.make_async_remote_copy(
            X1.at[h, i], X2.at[h, d2], top_s.at[2], top_r.at[2, h],
            device_id=(row(d0, i, rem(z2 + i, 2) + 2 * rem(z1 + div(i, 2), 2)), y), device_id_type=MESH,
        )

    def home(h):
        quarter = core + 2 * flip
        return out.at[:B, pl.ds(pl.multiple_of(quarter * B + h * W, W), W)]

    def f_copy(h, t):
        i = rem(d2 + t, 4)
        return pltpu.make_async_remote_copy(
            X2.at[h, i], home(h), top_s.at[3], top_r.at[3, h],
            device_id=(row(group + 2 * z0, d1, i), y), device_id_type=MESH,
        )

    def send(copy, h, own, local):
        for t in (1, 3, 2) if copy is b_copy else (2, 1, 3):
            copy(h, t).start()

        @pl.when(jnp.logical_not(own))
        def _():
            copy(h, 0).start()

        @pl.when(own)
        def _():
            local().start()

    prepare_first(core)
    sibling_wait(0)
    prepare_first(1 - core)
    for h in range(2):
        arrived(X0.at[h], top_r.at[0, h])
        apply(X0, h)
        send(b_copy, h, self_b, lambda: pltpu.make_async_copy(X0.at[h, kept_b], X1.at[h, d1], top_r.at[1, h]))
        if h == 0:
            ring_step(7, 0)
    ring_step(6, 1)
    ring_step(7, 1)
    arrived(PB.at[2, core, :, mine, :], pg_r.at[2])
    ring_step(6, 2)
    ring_step(7, 2)
    ring_begin(5)
    ring_step(6, 3)
    remainder(0)
    ring_step(7, 3)
    ring_step(5, 0)
    sibling_wait(1)
    prepare(1)


    ring_step(5, 1)
    for h in range(2):
        arrived(X1.at[h], top_r.at[1, h])
        apply(X1, h)
        send(c_copy, h, self_c, lambda: pltpu.make_async_copy(X1.at[h, d1], X2.at[h, d2], top_r.at[2, h]))
        if h == 0:
            for t in range(2, 4):
                ring_step(5, t)
            remainder(1)
    sibling_wait(2)
    prepare(2)

    for h in range(2):
        arrived(X2.at[h], top_r.at[2, h])
        apply(X2, h)
        send(f_copy, h, self_d, lambda: pltpu.make_async_copy(X2.at[h, d2], home(h), top_r.at[3, h]))

    for h in range(2):
        arrived(out.at[:B, 0 : 4 * W], top_r.at[3, h])

    for q in range(8):
        rows = pl.ds(0, 7 * S)
        arrived(LB.at[q, rows] if q < 3 else PB.at[0, 0, 0 : 4 if q == 5 else 2, rows], ring_s.at[q])
    for q in SHARED:
        arrived(PB.at[0, 0, 0 : 4 if q == 5 else 2], sib_s.at[q])
    arrived(WS.at[0:3], pg_s.at[0])
    arrived(X0.at[:, 0:3], top_s.at[0])
    for own, sem, few, all_ in (
        (self_a, pg_s.at[1], WS.at[0:3], WS.at[0:4]),
        (self_b, top_s.at[1], X0.at[:, 0:3], X0),
        (self_c, top_s.at[2], X1.at[:, 0:3], X1),
        (self_d, pg_s.at[2], WS.at[0:3], WS.at[0:4]),
        (self_d, top_s.at[3], X2.at[:, 0:3], X2),
    ):

        @pl.when(own)
        def _():
            arrived(few, sem)

        @pl.when(jnp.logical_not(own))
        def _():
            arrived(all_, sem)


def per_device(trailing, reflectors, leaf_factor, node_reflect, node_factor):
    anywhere = pl.BlockSpec(memory_space=pl.ANY)
    dma = pltpu.SemaphoreType.DMA
    tops = pltpu.VMEM((2, 4, B, W), F32)
    nodes = pltpu.VMEM((4, 2 * B, B), BF16)
    return pl.pallas_call(
        kernel,
        out_shape=pltpu.VMEM(trailing.shape, F32),
        in_specs=[anywhere] * 5,
        out_specs=pl.BlockSpec(memory_space=pltpu.VMEM),
        scratch_shapes=[
            pltpu.VMEM((6, S, B), F32),
            pltpu.VMEM((3, B, B), F32),
            pltpu.VMEM((3, 2, 4, B, B), F32),
            pltpu.VMEM((4, 2 * B, B), F32),
            pltpu.VMEM((4, 2, B, W), F32),
            pltpu.VMEM((4, 2, B, W), F32),
            tops, tops, tops,
            pltpu.VMEM((2, 2 * B, B), BF16),
            pltpu.VMEM((2, 2 * B, B), BF16),
            pltpu.VMEM((2 * B, B), BF16),
            nodes, nodes, nodes,
            dma((2,)), dma,
            dma((8,)), dma((8, 2, 4)),
            dma((3,)), dma((3,)),
            dma((8,)), dma((8,)),
            dma((4,)), dma((4, 2)),
        ],
        compiler_params=pltpu.CompilerParams(
            collective_id=0, has_side_effects=True, vmem_limit_bytes=56 * 1024 * 1024
        ),
        name="update",
    )(
        trailing,
        reflectors.T,
        leaf_factor.T,
        jnp.swapaxes(node_reflect, 1, 2),
        jnp.swapaxes(node_factor, 1, 2),
    )


def solution(mesh):
    in_specs = (
        P("row", "col"),
        P("row", "col"),
        P("row", "col"),
        P(None, "row", "col"),
        P(None, "row", "col"),
    )
    return jax.shard_map(
        per_device, mesh=mesh, in_specs=in_specs, out_specs=P("row", "col"), check_vma=False
    )
```
